32 devices in a mesh: dp: 8 (over z, x), tensor: 4 (over y, core).
Axes of the slice: x: 2, y: 2, z: 4, core: 2. Of those that a mesh axis runs over, the one named last changes fastest.
Arguments:
- block_input: float32 [8192, 768], P(('dp', 'tensor')), may hold values from -40 to 40
- norm_gain: float32 [768], replicated, may hold values from 0.5 to 1.5
- zx_weight: bfloat16 [2, 768, 1536], P(None, 'dp', 'tensor'), may hold values from -0.21875 to 0.21875
- bc_weight: bfloat16 [768, 256], P('dp'), may hold values from -0.21875 to 0.21875
- dt_weight: bfloat16 [768, 24], P('dp', 'tensor'), may hold values from -0.21875 to 0.21875
- conv_x_weight: float32 [4, 1536], replicated, may hold values from -3 to 3
- conv_x_bias: float32 [1536], replicated, may hold values from -0.5 to 0.5
- conv_bc_weight: float32 [4, 256], replicated, may hold values from -3 to 3
- conv_bc_bias: float32 [256], replicated, may hold values from -0.5 to 0.5
- dt_bias: float32 [24], replicated, may hold values from -7 to -2
- decay_log: float32 [24], replicated, may hold values from 0 to 1.5
- skip_gain: float32 [24], replicated, may hold values from 0.2 to 1
- gate_gain: float32 [1536], replicated, may hold values from 0.5 to 1.5
- out_weight: bfloat16 [1536, 768], P('tensor', 'dp'), may hold values from -0.15625 to 0.15625
- segments: int32 [8192], P('dp'), may hold values from 0 to 3, never falling along the last dimension, each value on 1 to 4096 neighbouring positions
- cotangent: float32 [8192, 768], P(('dp', 'tensor')), may hold values from -6 to 6
Outputs:
- output: float32 [8192, 768], P(('dp', 'tensor'))
- grad_input: float32 [8192, 768], P(('dp', 'tensor'))
- grad_norm_gain: float32 [768], replicated
- grad_zx_weight: float32 [2, 768, 1536], P(None, 'dp', 'tensor')
- grad_bc_weight: float32 [768, 256], P('dp')
- grad_dt_weight: float32 [768, 24], P('dp', 'tensor')
- grad_conv_x_weight: float32 [4, 1536], replicated
- grad_conv_x_bias: float32 [1536], replicated
- grad_conv_bc_weight: float32 [4, 256], replicated
- grad_conv_bc_bias: float32 [256], replicated
- grad_dt_bias: float32 [24], replicated
- grad_decay_log: float32 [24], replicated
- grad_skip_gain: float32 [24], replicated
- grad_gate_gain: float32 [1536], replicated
- grad_out_weight: float32 [1536, 768], P('tensor', 'dp')
The draws below stay inside these ranges and needn't reach their ends.
Inputs may be any that keep to these rules, and one draw needn't show every extreme that they name: `segments`: segment numbers never fall along the tokens and every number from 0 up occurs; a number covers at most 4096 consecutive tokens, and one covers exactly that many.
All inputs are finite; a program needn't handle non-finite values.
Results may differ from the reference program's by a relative error of at most 0.012.
The reference program's roundings to bfloat16 on the way (of `normed`, `pre`, `activ`, `normed_out`, `cot_b`, `d_gate_in`, `d_pre` and `d_raw_b`) count: a program that leaves them out, or rounds other values in their place, can miss the bound.
Values may be sent and summed in bfloat16 or wider, within the bound.
A program may use at most 256 MiB of HBM per device.

```python
import math
import jax
import jax.numpy as jnp
import numpy as np
from jax import lax

D = 768
H = 24
P_SIZE = 64
N = 128
KCONV = 4
GROUP = 256
LENGTH = 4096
TOK_DEV = 1024
DI = 1536
TOKENS = 8192


def draw_block_input(key, part):
    key_base, key_rows, key_cols = jax.random.split(key, 3)
    base = jnp.clip(jax.random.normal(key_base, (TOKENS, D), jnp.float32), -4.0, 4.0)
    row_scale = jnp.exp(jax.random.uniform(key_rows, (TOKENS, 1), jnp.float32, -1.15, 1.15))
    col_scale = jnp.exp(jax.random.uniform(key_cols, (1, D), jnp.float32, -1.15, 1.15))
    return base * row_scale * col_scale


def block_levels(key, extent, cuts, smallest, high):
    def one(axis_at, shards_of):
        draws = jax.random.uniform(jax.random.fold_in(jax.random.fold_in(key, 6), axis_at), (shards_of,), jnp.float32, smallest / len(cuts), high / len(cuts))
        return jnp.repeat(jnp.exp(draws), extent[axis_at] // shards_of).reshape((-1,) + (1,) * (len(extent) - axis_at - 1))

    gain = one(*cuts[0])
    for cut in cuts[1:]:
        gain = gain * one(*cut)
    return gain


def profile(amount, total, reach, skew):
    weights = [(1 << 20) // math.isqrt(grade ** skew) + 1 for grade in range(2, amount + 1)]
    surplus, counts = total - reach - (amount - 1), [1] * (amount - 1)
    while surplus > 0:
        free = [i for i in range(amount - 1) if counts[i] < reach]
        pool, budget = sum([weights[i] for i in free]), surplus
        for i in free:
            more = min(reach - counts[i], max(1, budget * weights[i] // pool), surplus)
            counts[i] = counts[i] + more
            surplus = surplus - more
    return np.array([reach] + counts)


def ragged(rng, count, total, bound, skew):
    if count == 2:
        one = jax.random.randint(rng, (), max(1, total - bound), min(bound, total - 1) + 1)
        return jnp.stack([one, total - one])
    lengths = jnp.asarray(profile(count, total, bound, skew), jnp.int32)
    pairs = (count - 1) // 2
    source_of, taker = lengths[1:1 + 2 * pairs:2], lengths[2:2 + 2 * pairs:2]
    margin = jnp.minimum(source_of - 1, bound - taker)
    shifted = jax.random.randint(jax.random.fold_in(rng, 1), (pairs,), 0, 1 << 20) % (margin + 1)
    lengths = lengths.at[1:1 + 2 * pairs:2].set(source_of - shifted).at[2:2 + 2 * pairs:2].set(taker + shifted)
    return lengths[jax.random.permutation(jax.random.fold_in(rng, 2), count)]


def normal_values(stream_key, extent, deviation, reach, cuts=(), kind=jnp.bfloat16):
    drawn = deviation * jax.random.normal(stream_key, extent, jnp.float32)
    if cuts:
        drawn = drawn * block_levels(stream_key, extent, cuts, -0.22, 0.18)
    return jnp.clip(drawn, -reach, reach).astype(kind)


def setup_inputs(seed: int = 0) -> dict:
    key_list = jax.random.split(jax.random.key(seed), 17)
    return {
        "block_input": draw_block_input(jax.random.fold_in(key_list[16], 71), 0),
        "norm_gain": jnp.clip(1.0 + 0.1 * jax.random.normal(key_list[1], (D,), jnp.float32), 0.5, 1.5),
        "zx_weight": normal_values(key_list[2], (2, D, DI), D ** -0.5, 0.21875, ((1, 8), (2, 4))),
        "bc_weight": normal_values(key_list[3], (D, 2 * N), D ** -0.5, 0.21875, ((0, 8),)),
        "dt_weight": normal_values(key_list[4], (D, H), D ** -0.5, 0.21875, ((0, 8), (1, 4))),
        "conv_x_weight": normal_values(key_list[5], (KCONV, DI), KCONV ** -0.5, 3.0, (), jnp.float32),
        "conv_x_bias": jnp.clip(jax.random.uniform(key_list[6], (DI,), jnp.float32, -0.5, 0.5), -0.5, 0.5),
        "conv_bc_weight": normal_values(key_list[7], (KCONV, 2 * N), KCONV ** -0.5, 3.0, (), jnp.float32),
        "conv_bc_bias": jnp.clip(jax.random.uniform(key_list[8], (2 * N,), jnp.float32, -0.5, 0.5), -0.5, 0.5),
        "dt_bias": jnp.clip(jax.random.uniform(key_list[9], (H,), jnp.float32, -7.0, -2.0), -7.0, -2.0),
        "decay_log": jnp.clip(jax.random.uniform(key_list[10], (H,), jnp.float32, 0.0, 1.5), 0.0, 1.5),
        "skip_gain": jnp.clip(jax.random.uniform(key_list[11], (H,), jnp.float32, 0.2, 1.0), 0.2, 1.0),
        "gate_gain": jnp.clip(1.0 + 0.1 * jax.random.normal(key_list[12], (DI,), jnp.float32), 0.5, 1.5),
        "out_weight": normal_values(key_list[13], (DI, D), DI ** -0.5, 0.15625, ((0, 4), (1, 8))),
        "segments": jnp.searchsorted(jnp.cumsum(ragged(key_list[14], TOKENS // (2 * TOK_DEV), TOKENS, 4 * TOK_DEV, 1)), jnp.arange(TOKENS), side="right").astype(jnp.int32),
        "cotangent": normal_values(key_list[15], (TOKENS, D), 1.0, 6.0, ((0, 32),), jnp.float32),
    }


EPSILON = 1e-05
exact_prec = lax.Precision.HIGHEST

def dot_wide(left, right):
    return jnp.dot(left, right, preferred_element_type=jnp.float32)

def ssd_groups(inner_x, state_b, state_c, step_dt, decay_log, resets, start_state):
    tokens_here = inner_x.shape[0]
    blocks = tokens_here // GROUP

    def to_blocks(array):
        return array.reshape((blocks, GROUP) + array.shape[1:])
    rate = -jnp.exp(decay_log)
    index = jnp.arange(GROUP, dtype=jnp.int32)
    lower = index[:, None] >= index[None, :]

    def advance(state, pieces):
        block_x, block_b, block_c, block_dt, block_reset = pieces
        log_decay = block_dt * rate[None, :]
        cumul = jnp.cumsum(log_decay, axis=0)
        run_id = jnp.cumsum(block_reset)
        same_run = (run_id[:, None] == run_id[None, :]) & lower
        spread = cumul[:, None, :] - cumul[None, :, :]
        mask_three = same_run[:, :, None]
        decay = jnp.where(mask_three, jnp.exp(jnp.where(mask_three, spread, 0.0)), 0.0)
        scores = jnp.dot(block_c, block_b.T, precision=exact_prec)
        weighted_x = block_x * block_dt[:, :, None]
        mixing = decay * scores[:, :, None]
        within = jnp.einsum('tsh,shp->thp', mixing, weighted_x, precision=exact_prec)
        keep_first = (run_id == 0).astype(jnp.float32)
        inflow_w = jnp.exp(cumul) * keep_first[:, None]
        carried = jnp.einsum('tn,hpn->thp', block_c, state, precision=exact_prec) * inflow_w[:, :, None]
        tail_w = decay[GROUP - 1]
        new_state = state * inflow_w[GROUP - 1][:, None, None] + jnp.einsum('sh,shp,sn->hpn', tail_w, weighted_x, block_b, precision=exact_prec)
        return (new_state, within + carried)
    final, outputs = lax.scan(advance, start_state, (to_blocks(inner_x), to_blocks(state_b), to_blocks(state_c), to_blocks(step_dt), to_blocks(resets)))
    return (outputs.reshape(inner_x.shape), final)

def conv_apply(pre_ext, kernel, offsets, validity):
    length = validity.shape[0]
    total = jnp.broadcast_to(offsets[None, :], (length, offsets.shape[0]))
    for offset in range(kernel.shape[0]):
        total = total + kernel[offset][None, :] * pre_ext[offset:offset + length] * validity[:, offset:offset + 1]
    return jax.nn.silu(total)

def valid_and_resets(seg_ext, pos_ext, width_back):
    length = seg_ext.shape[0] - width_back
    own_seg = seg_ext[width_back:]
    own_pos = pos_ext[width_back:]
    columns = []
    for offset in range(width_back + 1):
        same = (seg_ext[offset:offset + length] == own_seg) & (pos_ext[offset:offset + length] // LENGTH == own_pos // LENGTH)
        columns.append(same.astype(jnp.float32))
    validity = jnp.stack(columns, axis=1)
    resets = ((seg_ext[width_back - 1:width_back - 1 + length] != own_seg) | (own_pos % LENGTH == 0)).astype(jnp.float32)
    return (validity, resets)

def reference(block_input, norm_gain, zx_weight, bc_weight, dt_weight, conv_x_weight, conv_x_bias, conv_bc_weight, conv_bc_bias, dt_bias, decay_log, skip_gain, gate_gain, out_weight, segments, cotangent):
    width_back = conv_x_weight.shape[0] - 1
    seq_count = TOKENS // LENGTH
    conv_weight = jnp.concatenate([conv_x_weight, conv_bc_weight], axis=1)
    conv_bias = jnp.concatenate([conv_x_bias, conv_bc_bias])
    pos_ext = jnp.arange(LENGTH + width_back, dtype=jnp.int32) - width_back
    zero_state = jnp.zeros((H, P_SIZE, N), jnp.float32)

    def one_sequence(totals, pieces):
        resid, seg, cot = pieces
        rstd = lax.rsqrt(lax.optimization_barrier(jnp.mean(resid * resid, axis=-1, keepdims=True)) + EPSILON)
        normed = (resid * rstd * norm_gain).astype(jnp.bfloat16)
        gate_in = dot_wide(normed, zx_weight[0])
        pre = jnp.concatenate([dot_wide(normed, zx_weight[1]), dot_wide(normed, bc_weight)], axis=1).astype(jnp.bfloat16)
        raw_dt = dot_wide(normed, dt_weight) + dt_bias
        step_dt = jax.nn.softplus(raw_dt)
        seg_ext = jnp.concatenate([jnp.full((width_back,), -1, jnp.int32), seg.astype(jnp.int32)])
        validity, resets = valid_and_resets(seg_ext, pos_ext, width_back)
        pre_ext = jnp.concatenate([jnp.zeros((width_back, pre.shape[1]), jnp.float32), pre.astype(jnp.float32)], axis=0)
        activ = conv_apply(pre_ext, conv_weight, conv_bias, validity).astype(jnp.bfloat16)
        inner_x = activ[:, :DI].astype(jnp.float32).reshape(LENGTH, H, P_SIZE)
        state_b = activ[:, DI:DI + N].astype(jnp.float32)
        state_c = activ[:, DI + N:].astype(jnp.float32)

        def mixer(arg_x, arg_b, arg_c, arg_dt, arg_log):
            return ssd_groups(arg_x, arg_b, arg_c, arg_dt, arg_log, resets, zero_state)[0]
        scan_y, mixer_back = jax.vjp(mixer, inner_x, state_b, state_c, step_dt, decay_log)
        mixed_three = scan_y + skip_gain[None, :, None] * inner_x
        mixed = mixed_three.reshape(LENGTH, DI)
        gate_act = jax.nn.silu(gate_in)
        gated = mixed * gate_act
        rstd_gate = lax.rsqrt(lax.optimization_barrier(jnp.mean(gated * gated, axis=-1, keepdims=True)) + EPSILON)
        normed_out = (gated * rstd_gate * gate_gain).astype(jnp.bfloat16)
        result = resid + dot_wide(normed_out, out_weight)
        cot_b = cot.astype(jnp.bfloat16)
        d_normed_out = dot_wide(cot_b, out_weight.T)
        g_out = dot_wide(normed_out.T, cot_b)
        g_gate = lax.optimization_barrier(jnp.sum(d_normed_out * gated * rstd_gate, axis=0))
        scaled = gate_gain * d_normed_out
        d_gated = rstd_gate * scaled - gated * rstd_gate ** 3 * lax.optimization_barrier(jnp.mean(scaled * gated, axis=-1, keepdims=True))
        sigm = jax.nn.sigmoid(gate_in)
        d_mixed = d_gated * gate_act
        d_gate_in = (d_gated * mixed * sigm * (1.0 + gate_in * (1.0 - sigm))).astype(jnp.bfloat16)
        d_mixed_three = d_mixed.reshape(LENGTH, H, P_SIZE)
        g_skip = lax.optimization_barrier(jnp.sum(d_mixed_three * inner_x, axis=(0, 2)))
        d_x, d_b, d_c, d_step, d_log = mixer_back(d_mixed_three)
        d_x = d_x + skip_gain[None, :, None] * d_mixed_three
        d_activ = jnp.concatenate([d_x.reshape(LENGTH, DI), d_b, d_c], axis=1)

        def conv_part(values, kernel, offsets):
            return conv_apply(values, kernel, offsets, validity)
        conv_out, conv_back = jax.vjp(conv_part, pre_ext, conv_weight, conv_bias)
        d_pre_ext, g_conv_w, g_conv_b = conv_back(d_activ)
        d_pre = d_pre_ext[width_back:].astype(jnp.bfloat16)
        d_raw = d_step * jax.nn.sigmoid(raw_dt)
        g_dt_bias = lax.optimization_barrier(jnp.sum(d_raw, axis=0))
        d_raw_b = d_raw.astype(jnp.bfloat16)
        d_normed = dot_wide(d_gate_in, zx_weight[0].T) + dot_wide(d_pre[:, :DI], zx_weight[1].T) + dot_wide(d_pre[:, DI:], bc_weight.T) + dot_wide(d_raw_b, dt_weight.T)
        g_zx = jnp.stack([dot_wide(normed.T, d_gate_in), dot_wide(normed.T, d_pre[:, :DI])])
        g_bc = dot_wide(normed.T, d_pre[:, DI:])
        g_dt = dot_wide(normed.T, d_raw_b)
        scaled_in = norm_gain * d_normed
        g_norm = lax.optimization_barrier(jnp.sum(d_normed * resid * rstd, axis=0))
        d_resid = cot + rstd * scaled_in - resid * rstd ** 3 * lax.optimization_barrier(jnp.mean(scaled_in * resid, axis=-1, keepdims=True))
        parts = (g_norm, g_zx, g_bc, g_dt, g_conv_w, g_conv_b, g_dt_bias, d_log, g_skip, g_gate, g_out)
        new_totals = tuple((before + extra for before, extra in zip(totals, parts)))
        return (new_totals, (result, d_resid))
    start_totals = (jnp.zeros((D,), jnp.float32), jnp.zeros((2, D, DI), jnp.float32), jnp.zeros((D, 2 * N), jnp.float32), jnp.zeros((D, H), jnp.float32), jnp.zeros((KCONV, DI + 2 * N), jnp.float32), jnp.zeros((DI + 2 * N,), jnp.float32), jnp.zeros((H,), jnp.float32), jnp.zeros((H,), jnp.float32), jnp.zeros((H,), jnp.float32), jnp.zeros((DI,), jnp.float32), jnp.zeros((DI, D), jnp.float32))
    totals, outputs = lax.scan(one_sequence, start_totals, (block_input.reshape(seq_count, LENGTH, D), segments.reshape(seq_count, LENGTH), cotangent.reshape(seq_count, LENGTH, D)))
    result = outputs[0].reshape(TOKENS, D)
    grad_input = outputs[1].reshape(TOKENS, D)
    g_norm, g_zx, g_bc, g_dt, g_conv_w, g_conv_b, g_dt_bias, g_log, g_skip, g_gate, g_out = totals
    return (result, grad_input, g_norm, g_zx, g_bc, g_dt, g_conv_w[:, :DI], g_conv_b[:DI], g_conv_w[:, DI:], g_conv_b[DI:], g_dt_bias, g_log, g_skip, g_gate, g_out)
```

```python
import functools
import jax
import jax.numpy as jnp
from jax import lax
from jax.experimental import pallas as pl
from jax.experimental.pallas import tpu as pltpu
from jax.sharding import PartitionSpec as P

GROUP = 256
exact_prec = lax.Precision.HIGHEST
PAD = 8


def dot_wide(left, right):
    return jnp.dot(left, right, preferred_element_type=jnp.float32)


def dot_exact(left, right):
    return jnp.dot(left, right, precision=exact_prec, preferred_element_type=jnp.float32)


def dot_nt(left, right):
    return lax.dot_general(left, right, (((1,), (1,)), ((), ())), preferred_element_type=jnp.float32)


def dot_tn(left, right):
    return lax.dot_general(left, right, (((0,), (0,)), ((), ())), preferred_element_type=jnp.float32)


def head_maps(inner, head_size):
    wide = (
        lax.broadcasted_iota(jnp.int32, (PAD, inner), 1) // head_size
        == lax.broadcasted_iota(jnp.int32, (PAD, inner), 0)
    ).astype(jnp.float32)
    tall = (
        lax.broadcasted_iota(jnp.int32, (inner, PAD), 0) // head_size
        == lax.broadcasted_iota(jnp.int32, (inner, PAD), 1)
    ).astype(jnp.float32)
    return wide, tall


def block_terms(rows, la_ref, lat_ref, key_ref, keyt_ref, before):
    size = rows.size
    row_i = lax.broadcasted_iota(jnp.int32, (size, size), 0)
    col_i = lax.broadcasted_iota(jnp.int32, (size, size), 1)
    lower = row_i >= col_i
    lower_f = lower.astype(jnp.float32)
    upper_f = (row_i <= col_i).astype(jnp.float32)
    la = la_ref[rows, :]
    cum = dot_exact(lower_f, la)
    cumt = dot_exact(lat_ref[:, rows], upper_f)
    key = key_ref[rows, :]
    keyt = keyt_ref[:, rows]
    same = lower & (key == keyt)
    last_key = key[size - 1 :, :]
    last = cum[size - 1 :, :]
    inflow = jnp.where(key == before, jnp.exp(cum), 0.0)
    tail = jnp.where(key == last_key, jnp.exp(last - cum), 0.0)
    passing = jnp.where(last_key == before, jnp.exp(last), 0.0)
    passing_t = jnp.where(last_key == before, jnp.exp(cumt[:, size - 1 :]), 0.0)
    return cum, cumt, same, inflow, tail, passing, passing_t, last_key


def head_decay(same, cum, cumt, head):
    spread = jnp.where(same, cum[:, head : head + 1] - cumt[head : head + 1, :], -1e30)
    return jnp.exp(spread)


def scan_forward_kernel(
    heads, head_size, size, x_ref, b_ref, c_ref, dt_ref, dtt_ref, la_ref, lat_ref, key_ref,
    keyt_ref, before_ref, y_ref, end_ref, inflow_ref,
):
    tokens, inner = x_ref.shape
    wide, tall = head_maps(inner, head_size)
    end_ref[...] = jnp.zeros_like(end_ref)
    first_before = before_ref[...]

    def step(index, carry):
        before, total = carry
        rows = pl.ds(pl.multiple_of(index * size, size), size)
        cum, cumt, same, inflow, tail, passing, passing_t, last_key = block_terms(
            rows, la_ref, lat_ref, key_ref, keyt_ref, before
        )
        x, b, c = x_ref[rows, :], b_ref[rows, :], c_ref[rows, :]
        scores = dot_nt(c, b)
        state = end_ref[...]
        carried = dot_nt(c, state.astype(jnp.bfloat16)) * dot_exact(inflow, wide)
        for head in range(heads):
            cols = slice(head * head_size, (head + 1) * head_size)
            mixing = (
                scores * head_decay(same, cum, cumt, head) * dtt_ref[head : head + 1, rows]
            ).astype(jnp.bfloat16)
            y_ref[rows, cols] = dot_wide(mixing, x[:, cols]) + carried[:, cols]
        pushed = (x.astype(jnp.float32) * dot_exact(tail * dt_ref[rows, :], wide)).astype(
            jnp.bfloat16
        )
        end_ref[...] = state * dot_exact(tall, passing_t) + dot_tn(pushed, b)
        reach = jnp.where(key_ref[rows, :] == first_before, jnp.exp(cum + total), 0.0)
        inflow_ref[rows, :] = dot_exact(reach, wide)
        return last_key, total + cum[size - 1 :, :]

    lax.fori_loop(0, tokens // size, step, (first_before, jnp.zeros((1, PAD), jnp.float32)))


def scan_backward_kernel(
    heads, head_size, size, x_ref, b_ref, c_ref, dy_ref, dt_ref, dtt_ref, la_ref, lat_ref,
    key_ref, keyt_ref, before_ref, skip_ref, entry_ref, exit_ref,
    dx_ref, db_ref, dc_ref, dcum_ref, colt_ref, const_ref, sx_ref, states, cot,
):
    tokens, inner = x_ref.shape
    blocks = tokens // size
    wide, tall = head_maps(inner, head_size)
    states[0] = entry_ref[...]
    first_before = before_ref[...]

    def block_before(index):
        if isinstance(index, int) and index == 0:
            return first_before
        return key_ref[pl.ds(index * size - 1, 1), :]

    def block_rows(index):
        return pl.ds(index * size, size)

    for index in range(blocks - 1):
        rows = block_rows(index)
        terms = block_terms(rows, la_ref, lat_ref, key_ref, keyt_ref, block_before(index))
        tail, passing_t = terms[4], terms[6]
        pushed = (
            x_ref[rows, :].astype(jnp.float32) * dot_exact(tail * dt_ref[rows, :], wide)
        ).astype(jnp.bfloat16)
        states[index + 1] = states[index] * dot_exact(tall, passing_t) + dot_tn(
            pushed, b_ref[rows, :]
        )
    cot[...] = exit_ref[...]

    def step(turn, carry):
        index = blocks - 1 - turn
        rows = pl.ds(pl.multiple_of(index * size, size), size)
        prior = key_ref[pl.ds(jnp.maximum(index * size - 1, 0), 1), :]
        before = jnp.where(index == 0, first_before, prior)
        cum, cumt, same, inflow, tail, passing, passing_t, last_key = block_terms(
            rows, la_ref, lat_ref, key_ref, keyt_ref, before
        )
        strict = lax.broadcasted_iota(jnp.int32, (size, size), 0) > lax.broadcasted_iota(
            jnp.int32, (size, size), 1
        )
        x, b, c = x_ref[rows, :], b_ref[rows, :], c_ref[rows, :]
        x_wide = x.astype(jnp.float32)
        dy = dy_ref[rows, :]
        dy_low = dy.astype(jnp.bfloat16)
        dt = dt_ref[rows, :]
        state, grad = states[index], cot[...]
        state_low, grad_low = state.astype(jnp.bfloat16), grad.astype(jnp.bfloat16)
        scores = dot_nt(c, b)
        from_state = dot_nt(c, state_low)
        from_grad = dot_nt(b, grad_low)
        tail_wide = dot_exact(tail, wide)
        dt_wide = dot_exact(dt, wide)
        d_in = (dy * dot_exact(inflow, wide)).astype(jnp.bfloat16)
        pushed = (x_wide * tail_wide * dt_wide).astype(jnp.bfloat16)
        d_scores = jnp.zeros((size, size), jnp.float32)
        dxd = []
        row_sums = []
        for head in range(heads):
            cols = slice(head * head_size, (head + 1) * head_size)
            decay = head_decay(same, cum, cumt, head)
            mixing = scores * decay
            both = dot_nt(dy_low[:, cols], x[:, cols]) * dtt_ref[head : head + 1, rows]
            d_scores = d_scores + both * decay
            joint = jnp.where(strict, both * mixing, 0.0)
            row_sums.append(jnp.sum(joint, axis=1, keepdims=True))
            colt_ref[head : head + 1, rows] = jnp.sum(joint, axis=0, keepdims=True)
            dxd.append(dot_tn(mixing.astype(jnp.bfloat16), dy_low[:, cols]))
        for head in range(heads, PAD):
            row_sums.append(jnp.zeros((size, 1), jnp.float32))
            colt_ref[head : head + 1, rows] = jnp.zeros((1, size), jnp.float32)
        dxd = jnp.concatenate(dxd, axis=1) + from_grad * tail_wide
        sx_ref[rows, :] = dot_exact(dxd * x_wide, tall)
        dx_ref[rows, :] = dxd * dt_wide + dy * skip_ref[...]
        d_low = d_scores.astype(jnp.bfloat16)
        dc_ref[rows, :] = dot_wide(d_low, b) + dot_wide(d_in, state_low)
        db_ref[rows, :] = dot_tn(d_low, c) + dot_wide(pushed, grad_low)
        through = dot_exact(dy * from_state, tall) * inflow
        kept = dot_exact(x_wide * from_grad, tall) * tail * dt
        dcum_ref[rows, :] = jnp.concatenate(row_sums, axis=1) + through - kept
        whole = dot_exact(jnp.sum(state * grad, axis=1, keepdims=True).T, tall)
        const_ref[rows, :] = jnp.broadcast_to(
            jnp.sum(kept, axis=0, keepdims=True) + passing * whole, (size, PAD)
        )
        cot[...] = grad * dot_exact(tall, passing_t) + dot_tn(d_in, c)
        return carry

    lax.fori_loop(0, blocks, step, 0)


def vmem(count):
    return [pl.BlockSpec(memory_space=pltpu.VMEM)] * count


def scan_forward(x, b, c, dt, dtt, la, lat, key, keyt, before, heads):
    tokens, inner = x.shape
    size = min(GROUP, tokens)
    return pl.pallas_call(
        functools.partial(scan_forward_kernel, heads, inner // heads, size),
        out_shape=(
            jax.ShapeDtypeStruct((tokens, inner), jnp.float32),
            jax.ShapeDtypeStruct((inner, b.shape[1]), jnp.float32),
            jax.ShapeDtypeStruct((tokens, inner), jnp.float32),
        ),
        in_specs=vmem(10),
        out_specs=tuple(vmem(3)),
        compiler_params=pltpu.CompilerParams(vmem_limit_bytes=40 * 2**20),
        name="scan_forward",
    )(x, b, c, dt, dtt, la, lat, key, keyt, before)


def scan_backward(
    x, b, c, dy, dt, dtt, la, lat, key, keyt, before, skip, entry, leave, heads
):
    tokens, inner = x.shape
    size = min(GROUP, tokens)
    wide = b.shape[1]
    return pl.pallas_call(
        functools.partial(scan_backward_kernel, heads, inner // heads, size),
        out_shape=(
            jax.ShapeDtypeStruct((tokens, inner), jnp.float32),
            jax.ShapeDtypeStruct((tokens, wide), jnp.float32),
            jax.ShapeDtypeStruct((tokens, wide), jnp.float32),
            jax.ShapeDtypeStruct((tokens, PAD), jnp.float32),
            jax.ShapeDtypeStruct((PAD, tokens), jnp.float32),
            jax.ShapeDtypeStruct((tokens, PAD), jnp.float32),
            jax.ShapeDtypeStruct((tokens, PAD), jnp.float32),
        ),
        in_specs=vmem(14),
        out_specs=tuple(vmem(7)),
        scratch_shapes=[
            pltpu.VMEM((tokens // size, inner, wide), jnp.float32),
            pltpu.VMEM((inner, wide), jnp.float32),
        ],
        compiler_params=pltpu.CompilerParams(vmem_limit_bytes=48 * 2**20),
        name="scan_backward",
    )(x, b, c, dy, dt, dtt, la, lat, key, keyt, before, skip, entry, leave)


def step_gradients(dcum, colt, const, sx, dt, la, rate):
    tokens = dcum.shape[0]
    size = min(GROUP, tokens)
    change = (dcum - colt.T).reshape(tokens // size, size, PAD)
    index = jnp.arange(size, dtype=jnp.int32)
    upper = (index[:, None] <= index[None, :]).astype(jnp.float32)
    d_la = jnp.einsum("ts,bsh->bth", upper, change, precision=exact_prec).reshape(tokens, PAD)
    d_la = d_la + const
    return d_la * rate + sx, jnp.sum(d_la * la, axis=0)


LENGTH = 4096
EPSILON = 1e-05


def from_behind(block, axis, distance):
    devices = range(lax.axis_size(axis))
    route = [(i - distance, i) for i in devices if i - distance in devices]
    return lax.ppermute(block, axis, route)


def conv_apply(pre_ext, kernel, offsets, validity):
    length = validity.shape[0]
    total = jnp.broadcast_to(offsets[None, :], (length, offsets.shape[0]))
    for offset in range(kernel.shape[0]):
        total = (
            total
            + kernel[offset][None, :]
            * pre_ext[offset : offset + length]
            * validity[:, offset : offset + 1]
        )
    return jax.nn.silu(total)


def place_slice(piece, total_len, start, axis):
    full_shape = list(piece.shape)
    full_shape[axis] = total_len
    return lax.dynamic_update_slice_in_dim(
        jnp.zeros(tuple(full_shape), jnp.float32), piece, start, axis
    )


def pad_to(array, size, axis):
    widths = [(0, 0)] * array.ndim
    widths[axis] = (0, size - array.shape[axis])
    return jnp.pad(array, widths)


def chain(values, decays, mine, backward):
    count = values.shape[0]
    running = jnp.zeros(values.shape[1:], jnp.float32)
    order = range(count - 1, 0, -1) if backward else range(count - 1)
    for index in order:
        longer = running * decays[index] + values[index].astype(jnp.float32)
        reached = index > mine if backward else index < mine
        running = jnp.where(reached, longer, running)
    return running


def per_device(
    block_input,
    norm_gain,
    zx_weight,
    bc_weight,
    dt_weight,
    conv_x_weight,
    conv_x_bias,
    conv_bc_weight,
    conv_bc_bias,
    dt_bias,
    decay_log,
    skip_gain,
    gate_gain,
    out_weight,
    segments,
    cotangent,
):
    low = jnp.bfloat16
    tensor_count = lax.axis_size("tensor")
    tensor_index = lax.axis_index("tensor")
    data_count = lax.axis_size("dp")
    data_index = lax.axis_index("dp")
    token_count = segments.shape[0]
    row_count, width = block_input.shape
    part = zx_weight.shape[1]
    heads_here = dt_weight.shape[1]
    inner_here = out_weight.shape[0]
    head_size = inner_here // heads_here
    inner_total = inner_here * tensor_count
    heads_total = heads_here * tensor_count
    width_back = conv_x_weight.shape[0] - 1
    bc_size = bc_weight.shape[1]
    state_size = bc_size // 2
    head_start = tensor_index * heads_here
    inner_start = tensor_index * inner_here

    def own_heads(array):
        return pad_to(lax.dynamic_slice_in_dim(array, head_start, heads_here), PAD, 0)

    local_bias, local_log, local_skip = map(own_heads, (dt_bias, decay_log, skip_gain))
    local_gate_gain = lax.dynamic_slice_in_dim(gate_gain, inner_start, inner_here)
    skip_wide = jnp.repeat(local_skip[:heads_here], head_size)[None, :]
    conv_weight = jnp.concatenate(
        [lax.dynamic_slice_in_dim(conv_x_weight, inner_start, inner_here, 1), conv_bc_weight],
        axis=1,
    )
    conv_bias = jnp.concatenate(
        [lax.dynamic_slice_in_dim(conv_x_bias, inner_start, inner_here), conv_bc_bias]
    )
    rstd = lax.rsqrt(jnp.mean(block_input * block_input, axis=-1, keepdims=True) + EPSILON)
    normed_rows = (block_input * rstd * norm_gain).astype(low)
    normed = lax.all_gather(normed_rows, "tensor", axis=0, tiled=True)
    extra_size = -(-(bc_size + PAD) // 128) * 128
    side = jnp.concatenate([bc_weight, dt_weight], axis=1)
    side = pad_to(side, max(extra_size, inner_here), 1)
    packed = jnp.stack([zx_weight[0], zx_weight[1], side, out_weight.T])
    every = lax.all_gather(packed, "dp", axis=1, tiled=True)
    w_gate, w_mix, w_side, w_out = every[0], every[1], every[2], every[3]
    cot_full = lax.all_gather(cotangent.astype(low), "tensor", axis=0, tiled=True)

    gate_in = dot_wide(normed, w_gate)
    side_out = dot_wide(normed, w_side)
    pre = jnp.concatenate([dot_wide(normed, w_mix), side_out[:, :bc_size]], axis=1).astype(low)
    raw_dt = side_out[:, bc_size : bc_size + PAD] + local_bias
    step_dt = jax.nn.softplus(raw_dt)
    rate = -jnp.exp(local_log) * (jnp.arange(PAD) < heads_here)
    log_decay = step_dt * rate

    tail_start = token_count - width_back
    own_tail = jnp.concatenate(
        [pre[tail_start:], segments[tail_start:, None].astype(low)], axis=1
    )
    tail = from_behind(own_tail, "dp", 1)
    tail_vals, tail_ids = tail[:, :-1], tail[:, -1].astype(jnp.int32)
    seg_ext = jnp.concatenate([tail_ids, segments])
    pos_ext = (
        data_index * token_count
        - width_back
        + jnp.arange(token_count + width_back, dtype=jnp.int32)
    )
    sequences = data_count * token_count // LENGTH + 1
    key_ext = seg_ext * sequences + pos_ext // LENGTH
    key = key_ext[width_back:]
    before = key_ext[width_back - 1 : width_back].reshape(1, 1)
    validity = jnp.stack(
        [key_ext[k : k + token_count] == key for k in range(width_back + 1)], axis=1
    ).astype(jnp.float32)
    pre_ext = jnp.concatenate([tail_vals, pre], axis=0).astype(jnp.float32)
    activ = conv_apply(pre_ext, conv_weight, conv_bias, validity).astype(low)
    inner_x = activ[:, :inner_here]
    state_b = activ[:, inner_here : inner_here + state_size]
    state_c = activ[:, inner_here + state_size :]
    scan_args = (
        step_dt, step_dt.T, log_decay, log_decay.T, key[:, None], key[None, :], before,
    )
    local_y, local_end, inflow = scan_forward(
        inner_x, state_b, state_c, *scan_args, heads=heads_here
    )

    group = max(1, LENGTH // token_count)
    if data_count % group:
        group = data_count
    lines = [list(range(i, i + group)) for i in range(0, data_count, group)]
    mine = data_index % group

    def gather_line(array):
        return lax.all_gather(array, "dp", axis_index_groups=lines)

    device_decay = jnp.repeat(inflow[-1].reshape(heads_here, head_size)[:, :1], state_size, axis=1)
    sent = jnp.concatenate([local_end.astype(low), pad_to(device_decay, 16, 0).astype(low)])
    arrived = gather_line(sent)
    decays = jnp.repeat(
        arrived[:, inner_here : inner_here + heads_here].astype(jnp.float32), head_size, axis=1
    )
    entry_state = chain(arrived[:, :inner_here], decays, mine, False)
    x_wide = inner_x.astype(jnp.float32)
    mixed = (
        local_y + dot_wide(state_c, entry_state.T.astype(low)) * inflow + skip_wide * x_wide
    )
    sigm = jax.nn.sigmoid(gate_in)
    gate_act = gate_in * sigm
    gated = mixed * gate_act
    d_normed_out = dot_wide(cot_full, w_out)
    scaled = local_gate_gain * d_normed_out
    sums = jnp.stack([jnp.sum(gated * gated, axis=1), jnp.sum(scaled * gated, axis=1)])
    sums = lax.psum(sums, "tensor") / inner_total
    rstd_gate = lax.rsqrt(sums[0] + EPSILON)[:, None]
    gate_dots = sums[1][:, None]
    gated_normed = gated * rstd_gate
    normed_out = (gated_normed * local_gate_gain).astype(low)
    d_gated = rstd_gate * scaled - gated * rstd_gate**3 * gate_dots
    d_mixed = d_gated * gate_act
    state_cot = dot_wide((d_mixed * inflow).T.astype(low), state_c)
    cots = gather_line(state_cot.astype(low))
    leave_cot = chain(cots, decays, mine, True)
    branch = lax.psum_scatter(
        dot_wide(normed_out, w_out.T).astype(low), "tensor", scatter_dimension=0, tiled=True
    )
    result = block_input + branch.astype(jnp.float32)
    g_out = dot_wide(cot_full.T, normed_out).astype(low)
    g_out = lax.psum_scatter(g_out, "dp", scatter_dimension=0, tiled=True)
    g_gate_local = jnp.sum(d_normed_out * gated_normed, axis=0)
    d_gate_in = (d_gated * mixed * sigm * (1.0 + gate_in * (1.0 - sigm))).astype(low)
    g_skip_wide = jnp.sum(d_mixed * x_wide, axis=0)
    g_skip_local = jnp.sum(g_skip_wide.reshape(heads_here, head_size), axis=1)

    d_x, d_b, d_c, dcum, colt, const, sx = scan_backward(
        inner_x, state_b, state_c, d_mixed, *scan_args, skip_wide, entry_state, leave_cot,
        heads=heads_here,
    )
    d_bc = lax.psum(jnp.concatenate([d_b, d_c], axis=1).astype(low), "tensor")
    d_step, d_log = step_gradients(dcum, colt, const, sx, step_dt, log_decay, rate)
    d_activ = jnp.concatenate([d_x, d_bc.astype(jnp.float32)], axis=1)

    def conv_part(values, kernel, offsets):
        return conv_apply(values, kernel, offsets, validity)

    conv_out, conv_back = jax.vjp(conv_part, pre_ext, conv_weight, conv_bias)
    d_pre_ext, g_conv_w, g_conv_b = conv_back(d_activ)
    from_next = from_behind(d_pre_ext[:width_back], "dp", -1)
    d_pre_own = d_pre_ext[width_back:]
    d_pre = jnp.concatenate(
        [d_pre_own[:tail_start], d_pre_own[tail_start:] + from_next], axis=0
    ).astype(low)
    d_raw = d_step * jax.nn.sigmoid(raw_dt)
    g_dt_bias_local = jnp.sum(d_raw, axis=0)
    d_raw_b = d_raw.astype(low)
    d_mix = d_pre[:, :inner_here]
    d_side = jnp.concatenate([d_pre[:, inner_here:], d_raw_b], axis=1)
    partial_rows = (
        dot_wide(d_gate_in, w_gate.T)
        + dot_wide(d_mix, w_mix.T)
        + dot_wide(d_raw_b, w_side[:, bc_size : bc_size + PAD].T)
    )
    own_bc = lax.dynamic_slice_in_dim(d_pre[:, inner_here:], tensor_index * row_count, row_count, 0)
    d_normed_rows = lax.psum_scatter(
        partial_rows.astype(low), "tensor", scatter_dimension=0, tiled=True
    ).astype(jnp.float32) + dot_wide(own_bc, w_side[:, :bc_size].T)
    g_in = jnp.stack(
        [
            dot_wide(normed.T, d_gate_in),
            dot_wide(normed.T, d_mix),
            pad_to(dot_wide(normed.T, d_side), inner_here, 1),
        ]
    ).astype(low)
    g_in = lax.psum_scatter(g_in, "dp", scatter_dimension=1, tiled=True).astype(jnp.float32)
    grad_zx = g_in[:2]
    grad_bc = g_in[2, :, :bc_size]
    grad_dt = g_in[2, :, bc_size : bc_size + heads_here]
    grad_out = g_out.astype(jnp.float32).T
    scaled_in = norm_gain * d_normed_rows
    g_norm_local = jnp.sum(d_normed_rows * block_input * rstd, axis=0)
    grad_input = (
        cotangent
        + rstd * scaled_in
        - block_input * rstd**3 * jnp.mean(scaled_in * block_input, axis=-1, keepdims=True)
    )
    pieces = (
        g_norm_local,
        place_slice(g_conv_w[:, :inner_here], inner_total, inner_start, 1),
        place_slice(g_conv_b[:inner_here], inner_total, inner_start, 0),
        g_conv_w[:, inner_here:] / tensor_count,
        g_conv_b[inner_here:] / tensor_count,
        place_slice(g_dt_bias_local[:heads_here], heads_total, head_start, 0),
        place_slice(d_log[:heads_here], heads_total, head_start, 0),
        place_slice(g_skip_local, heads_total, head_start, 0),
        place_slice(g_gate_local, inner_total, inner_start, 0),
    )
    flat = jnp.concatenate([piece.reshape(-1) for piece in pieces])
    flat = pad_to(flat, -(-flat.shape[0] // 1024) * 1024, 0)
    flat = lax.psum(flat, ("dp", "tensor"))
    small, at = [], 0
    for piece in pieces:
        small.append(flat[at : at + piece.size].reshape(piece.shape))
        at += piece.size
    grad_norm, grad_cxw, grad_cxb, grad_cbw, grad_cbb, grad_dtb, grad_log, grad_skip, grad_gate = (
        small
    )
    return (
        result,
        grad_input,
        grad_norm,
        grad_zx,
        grad_bc,
        grad_dt,
        grad_cxw,
        grad_cxb,
        grad_cbw,
        grad_cbb,
        grad_dtb,
        grad_log,
        grad_skip,
        grad_gate,
        grad_out,
    )


def solution(mesh):
    in_specs = (
        P(("dp", "tensor"), None),
        P(),
        P(None, "dp", "tensor"),
        P("dp", None),
        P("dp", "tensor"),
        P(),
        P(),
        P(),
        P(),
        P(),
        P(),
        P(),
        P(),
        P("tensor", "dp"),
        P("dp"),
        P(("dp", "tensor"), None),
    )
    out_specs = (
        P(("dp", "tensor"), None),
        P(("dp", "tensor"), None),
        P(),
        P(None, "dp", "tensor"),
        P("dp", None),
        P("dp", "tensor"),
        P(),
        P(),
        P(),
        P(),
        P(),
        P(),
        P(),
        P(),
        P("tensor", "dp"),
    )
    return jax.shard_map(
        per_device, mesh=mesh, in_specs=in_specs, out_specs=out_specs, check_vma=False
    )
```

```python
import functools
import jax
import jax.numpy as jnp
from jax import lax
from jax.experimental import pallas as pl
from jax.experimental.pallas import tpu as pltpu
from jax.sharding import PartitionSpec as P


GROUP = 256
exact_prec = lax.Precision.HIGHEST
PAD = 8


def dot_wide(left, right):
    return jnp.dot(left, right, preferred_element_type=jnp.float32)


def dot_exact(left, right):
    return jnp.dot(left, right, precision=exact_prec, preferred_element_type=jnp.float32)


def dot_nt(left, right):
    return lax.dot_general(left, right, (((1,), (1,)), ((), ())), preferred_element_type=jnp.float32)


def dot_tn(left, right):
    return lax.dot_general(left, right, (((0,), (0,)), ((), ())), preferred_element_type=jnp.float32)


def head_maps(inner, head_size):
    wide = (
        lax.broadcasted_iota(jnp.int32, (PAD, inner), 1) // head_size
        == lax.broadcasted_iota(jnp.int32, (PAD, inner), 0)
    ).astype(jnp.float32)
    tall = (
        lax.broadcasted_iota(jnp.int32, (inner, PAD), 0) // head_size
        == lax.broadcasted_iota(jnp.int32, (inner, PAD), 1)
    ).astype(jnp.float32)
    return wide, tall


def block_terms(rows, la_ref, lat_ref, key_ref, keyt_ref, before):
    size = rows.size
    row_i = lax.broadcasted_iota(jnp.int32, (size, size), 0)
    col_i = lax.broadcasted_iota(jnp.int32, (size, size), 1)
    lower = row_i >= col_i
    lower_f = lower.astype(jnp.float32)
    upper_f = (row_i <= col_i).astype(jnp.float32)
    la = la_ref[rows, :]
    cum = dot_exact(lower_f, la)
    cumt = dot_exact(lat_ref[:, rows], upper_f)
    key = key_ref[rows, :]
    keyt = keyt_ref[:, rows]
    same = lower & (key == keyt)
    last_key = key[size - 1 :, :]
    last = cum[size - 1 :, :]
    inflow = jnp.where(key == before, jnp.exp(cum), 0.0)
    tail = jnp.where(key == last_key, jnp.exp(last - cum), 0.0)
    passing = jnp.where(last_key == before, jnp.exp(last), 0.0)
    passing_t = jnp.where(last_key == before, jnp.exp(cumt[:, size - 1 :]), 0.0)
    return cum, cumt, same, inflow, tail, passing, passing_t, last_key


def head_decay(same, cum, cumt, head):
    spread = jnp.where(same, cum[:, head : head + 1] - cumt[head : head + 1, :], -1e30)
    return jnp.exp(spread)


def scan_forward_kernel(
    heads, head_size, size, x_ref, b_ref, c_ref, dt_ref, dtt_ref, la_ref, lat_ref, key_ref,
    keyt_ref, before_ref, y_ref, end_ref, inflow_ref,
):
    tokens, inner = x_ref.shape
    wide, tall = head_maps(inner, head_size)
    end_ref[...] = jnp.zeros_like(end_ref)
    first_before = before_ref[...]

    def step(index, carry):
        before, total = carry
        rows = pl.ds(pl.multiple_of(index * size, size), size)
        cum, cumt, same, inflow, tail, _, passing_t, last_key = block_terms(
            rows, la_ref, lat_ref, key_ref, keyt_ref, before
        )
        x, b, c = x_ref[rows, :], b_ref[rows, :], c_ref[rows, :]
        scores = dot_nt(c, b)
        state = end_ref[...]
        carried = dot_nt(c, state.astype(jnp.bfloat16)) * dot_exact(inflow, wide)
        for head in range(heads):
            cols = slice(head * head_size, (head + 1) * head_size)
            mixing = (
                scores * head_decay(same, cum, cumt, head) * dtt_ref[head : head + 1, rows]
            ).astype(jnp.bfloat16)
            y_ref[rows, cols] = dot_wide(mixing, x[:, cols]) + carried[:, cols]
        pushed = (x.astype(jnp.float32) * dot_exact(tail * dt_ref[rows, :], wide)).astype(
            jnp.bfloat16
        )
        end_ref[...] = state * dot_exact(tall, passing_t) + dot_tn(pushed, b)
        reach = jnp.where(key_ref[rows, :] == first_before, jnp.exp(cum + total), 0.0)
        inflow_ref[rows, :] = dot_exact(reach, wide)
        return last_key, total + cum[size - 1 :, :]

    lax.fori_loop(0, tokens // size, step, (first_before, jnp.zeros((1, PAD), jnp.float32)))


def scan_backward_kernel(
    heads, head_size, size, x_ref, b_ref, c_ref, dy_ref, dt_ref, dtt_ref, la_ref, lat_ref,
    key_ref, keyt_ref, before_ref, skip_ref, entry_ref, exit_ref,
    dx_ref, db_ref, dc_ref, dcum_ref, colt_ref, const_ref, sx_ref, states, cot,
):
    tokens, inner = x_ref.shape
    blocks = tokens // size
    wide, tall = head_maps(inner, head_size)
    states[0] = entry_ref[...]
    first_before = before_ref[...]

    def block_before(index):
        if isinstance(index, int) and index == 0:
            return first_before
        return key_ref[pl.ds(index * size - 1, 1), :]

    def block_rows(index):
        return pl.ds(index * size, size)

    for index in range(blocks - 1):
        rows = block_rows(index)
        terms = block_terms(rows, la_ref, lat_ref, key_ref, keyt_ref, block_before(index))
        tail, passing_t = terms[4], terms[6]
        pushed = (
            x_ref[rows, :].astype(jnp.float32) * dot_exact(tail * dt_ref[rows, :], wide)
        ).astype(jnp.bfloat16)
        states[index + 1] = states[index] * dot_exact(tall, passing_t) + dot_tn(
            pushed, b_ref[rows, :]
        )
    cot[...] = exit_ref[...]

    def step(turn, carry):
        index = blocks - 1 - turn
        rows = pl.ds(pl.multiple_of(index * size, size), size)
        prior = key_ref[pl.ds(jnp.maximum(index * size - 1, 0), 1), :]
        before = jnp.where(index == 0, first_before, prior)
        cum, cumt, same, inflow, tail, passing, passing_t, _ = block_terms(
            rows, la_ref, lat_ref, key_ref, keyt_ref, before
        )
        strict = lax.broadcasted_iota(jnp.int32, (size, size), 0) > lax.broadcasted_iota(
            jnp.int32, (size, size), 1
        )
        x, b, c = x_ref[rows, :], b_ref[rows, :], c_ref[rows, :]
        x_wide = x.astype(jnp.float32)
        dy = dy_ref[rows, :]
        dy_low = dy.astype(jnp.bfloat16)
        dt = dt_ref[rows, :]
        state, grad = states[index], cot[...]
        state_low, grad_low = state.astype(jnp.bfloat16), grad.astype(jnp.bfloat16)
        scores = dot_nt(c, b)
        from_state = dot_nt(c, state_low)
        from_grad = dot_nt(b, grad_low)
        tail_wide = dot_exact(tail, wide)
        dt_wide = dot_exact(dt, wide)
        d_in = (dy * dot_exact(inflow, wide)).astype(jnp.bfloat16)
        pushed = (x_wide * tail_wide * dt_wide).astype(jnp.bfloat16)
        d_scores = jnp.zeros((size, size), jnp.float32)
        dxd = []
        row_sums = []
        for head in range(heads):
            cols = slice(head * head_size, (head + 1) * head_size)
            decay = head_decay(same, cum, cumt, head)
            mixing = scores * decay
            both = dot_nt(dy_low[:, cols], x[:, cols]) * dtt_ref[head : head + 1, rows]
            d_scores = d_scores + both * decay
            joint = jnp.where(strict, both * mixing, 0.0)
            row_sums.append(jnp.sum(joint, axis=1, keepdims=True))
            colt_ref[head : head + 1, rows] = jnp.sum(joint, axis=0, keepdims=True)
            dxd.append(dot_tn(mixing.astype(jnp.bfloat16), dy_low[:, cols]))
        for head in range(heads, PAD):
            row_sums.append(jnp.zeros((size, 1), jnp.float32))
            colt_ref[head : head + 1, rows] = jnp.zeros((1, size), jnp.float32)
        dxd = jnp.concatenate(dxd, axis=1) + from_grad * tail_wide
        sx_ref[rows, :] = dot_exact(dxd * x_wide, tall)
        dx_ref[rows, :] = dxd * dt_wide + dy * skip_ref[...]
        d_low = d_scores.astype(jnp.bfloat16)
        dc_ref[rows, :] = dot_wide(d_low, b) + dot_wide(d_in, state_low)
        db_ref[rows, :] = dot_tn(d_low, c) + dot_wide(pushed, grad_low)
        through = dot_exact(dy * from_state, tall) * inflow
        kept = dot_exact(x_wide * from_grad, tall) * tail * dt
        dcum_ref[rows, :] = jnp.concatenate(row_sums, axis=1) + through - kept
        whole = dot_exact(jnp.sum(state * grad, axis=1, keepdims=True).T, tall)
        const_ref[rows, :] = jnp.broadcast_to(
            jnp.sum(kept, axis=0, keepdims=True) + passing * whole, (size, PAD)
        )
        cot[...] = grad * dot_exact(tall, passing_t) + dot_tn(d_in, c)
        return carry

    lax.fori_loop(0, blocks, step, 0)


def vmem(count):
    return [pl.BlockSpec(memory_space=pltpu.VMEM)] * count


def scan_forward(x, b, c, dt, dtt, la, lat, key, keyt, before, heads):
    tokens, inner = x.shape
    size = min(GROUP, tokens)
    return pl.pallas_call(
        functools.partial(scan_forward_kernel, heads, inner // heads, size),
        out_shape=(
            jax.ShapeDtypeStruct((tokens, inner), jnp.float32),
            jax.ShapeDtypeStruct((inner, b.shape[1]), jnp.float32),
            jax.ShapeDtypeStruct((tokens, inner), jnp.float32),
        ),
        in_specs=vmem(10),
        out_specs=tuple(vmem(3)),
        compiler_params=pltpu.CompilerParams(vmem_limit_bytes=40 * 2**20),
        name="scan_forward",
    )(x, b, c, dt, dtt, la, lat, key, keyt, before)


def scan_backward(
    x, b, c, dy, dt, dtt, la, lat, key, keyt, before, skip, entry, leave, heads
):
    tokens, inner = x.shape
    size = min(GROUP, tokens)
    wide = b.shape[1]
    return pl.pallas_call(
        functools.partial(scan_backward_kernel, heads, inner // heads, size),
        out_shape=(
            jax.ShapeDtypeStruct((tokens, inner), jnp.float32),
            jax.ShapeDtypeStruct((tokens, wide), jnp.float32),
            jax.ShapeDtypeStruct((tokens, wide), jnp.float32),
            jax.ShapeDtypeStruct((tokens, PAD), jnp.float32),
            jax.ShapeDtypeStruct((PAD, tokens), jnp.float32),
            jax.ShapeDtypeStruct((tokens, PAD), jnp.float32),
            jax.ShapeDtypeStruct((tokens, PAD), jnp.float32),
        ),
        in_specs=vmem(14),
        out_specs=tuple(vmem(7)),
        scratch_shapes=[
            pltpu.VMEM((tokens // size, inner, wide), jnp.float32),
            pltpu.VMEM((inner, wide), jnp.float32),
        ],
        compiler_params=pltpu.CompilerParams(vmem_limit_bytes=48 * 2**20),
        name="scan_backward",
    )(x, b, c, dy, dt, dtt, la, lat, key, keyt, before, skip, entry, leave)


def step_gradients(dcum, colt, const, sx, la, rate):
    tokens = dcum.shape[0]
    size = min(GROUP, tokens)
    change = (dcum - colt.T).reshape(tokens // size, size, PAD)
    index = jnp.arange(size, dtype=jnp.int32)
    upper = (index[:, None] <= index[None, :]).astype(jnp.float32)
    d_la = jnp.einsum("ts,bsh->bth", upper, change, precision=exact_prec).reshape(tokens, PAD)
    d_la = d_la + const
    return d_la * rate + sx, jnp.sum(d_la * la, axis=0)


def spread_kernel(axis, group, own_ref, out_ref, send_sem, recv_sem):
    place = lax.axis_index(axis)
    mine = lax.rem(place, group)
    base = place - mine
    barrier = pltpu.get_barrier_semaphore()
    peers = [base + lax.rem(mine + k, group) for k in range(1, group)]
    for peer in peers:
        pl.semaphore_signal(
            barrier, inc=1, device_id={axis: peer}, device_id_type=pl.DeviceIdType.MESH
        )
    pl.semaphore_wait(barrier, group - 1)
    copies = []
    for k, peer in enumerate(peers):
        copy = pltpu.make_async_remote_copy(
            src_ref=own_ref,
            dst_ref=out_ref.at[mine],
            send_sem=send_sem.at[k],
            recv_sem=recv_sem.at[k],
            device_id={axis: peer},
            device_id_type=pl.DeviceIdType.MESH,
        )
        copy.start()
        copies.append(copy)
    out_ref[mine] = own_ref[...]
    for copy in copies:
        copy.wait()


def spread(array, axis, group, number):
    if group == 1:
        return array[None]
    return pl.pallas_call(
        functools.partial(spread_kernel, axis, group),
        out_shape=jax.ShapeDtypeStruct((group,) + array.shape, array.dtype),
        in_specs=vmem(1),
        out_specs=vmem(1)[0],
        scratch_shapes=[
            pltpu.SemaphoreType.DMA((group - 1,)),
            pltpu.SemaphoreType.DMA((group - 1,)),
        ],
        compiler_params=pltpu.CompilerParams(collective_id=number, has_side_effects=True),
    )(array)


LENGTH = 4096
EPSILON = 1e-05


def from_behind(block, axis, distance):
    devices = range(lax.axis_size(axis))
    route = [(i - distance, i) for i in devices if i - distance in devices]
    return lax.ppermute(block, axis, route)


def conv_apply(pre_ext, kernel, offsets, validity):
    length = validity.shape[0]
    total = jnp.broadcast_to(offsets[None, :], (length, offsets.shape[0]))
    for offset in range(kernel.shape[0]):
        total = (
            total
            + kernel[offset][None, :]
            * pre_ext[offset : offset + length]
            * validity[:, offset : offset + 1]
        )
    return jax.nn.silu(total)


def pad_to(array, size, axis):
    widths = [(0, 0)] * array.ndim
    widths[axis] = (0, size - array.shape[axis])
    return jnp.pad(array, widths)


def chain(values, decays, mine, backward):
    count = values.shape[0]
    running = jnp.zeros(values.shape[1:], jnp.float32)
    order = range(count - 1, 0, -1) if backward else range(count - 1)
    for index in order:
        longer = running * decays[index] + values[index].astype(jnp.float32)
        reached = index > mine if backward else index < mine
        running = jnp.where(reached, longer, running)
    return running


def per_device(
    block_input,
    norm_gain,
    zx_weight,
    bc_weight,
    dt_weight,
    conv_x_weight,
    conv_x_bias,
    conv_bc_weight,
    conv_bc_bias,
    dt_bias,
    decay_log,
    skip_gain,
    gate_gain,
    out_weight,
    segments,
    cotangent,
):
    low = jnp.bfloat16
    tensor_count = lax.axis_size("tensor")
    tensor_index = lax.axis_index("tensor")
    data_count = lax.axis_size("dp")
    data_index = lax.axis_index("dp")
    token_count = segments.shape[0]
    row_count, _ = block_input.shape
    heads_here = dt_weight.shape[1]
    inner_here = out_weight.shape[0]
    head_size = inner_here // heads_here
    inner_total = inner_here * tensor_count
    width_back = conv_x_weight.shape[0] - 1
    bc_size = bc_weight.shape[1]
    state_size = bc_size // 2
    head_start = tensor_index * heads_here
    inner_start = tensor_index * inner_here

    def own_heads(array):
        return pad_to(lax.dynamic_slice_in_dim(array, head_start, heads_here), PAD, 0)

    local_bias, local_log, local_skip = map(own_heads, (dt_bias, decay_log, skip_gain))
    local_gate_gain = lax.dynamic_slice_in_dim(gate_gain, inner_start, inner_here)
    skip_wide = jnp.repeat(local_skip[:heads_here], head_size)[None, :]
    conv_weight = jnp.concatenate(
        [lax.dynamic_slice_in_dim(conv_x_weight, inner_start, inner_here, 1), conv_bc_weight],
        axis=1,
    )
    conv_bias = jnp.concatenate(
        [lax.dynamic_slice_in_dim(conv_x_bias, inner_start, inner_here), conv_bc_bias]
    )
    rstd = lax.rsqrt(jnp.mean(block_input * block_input, axis=-1, keepdims=True) + EPSILON)
    normed_rows = (block_input * rstd * norm_gain).astype(low)
    normed = lax.all_gather(normed_rows, "tensor", axis=0, tiled=True)
    extra_size = -(-(bc_size + PAD) // 128) * 128
    side = jnp.concatenate([bc_weight, dt_weight], axis=1)
    side = pad_to(side, max(extra_size, inner_here), 1)
    packed = jnp.concatenate([zx_weight, side[None]])
    every = lax.all_gather(packed, "dp", axis=1, tiled=True)
    out_part, cot_rows, every, normed = lax.optimization_barrier(
        (out_weight.T, cotangent.astype(low), every, normed)
    )
    w_gate, w_mix, w_side = every[0], every[1], every[2]
    w_out = lax.all_gather(out_part, "dp", axis=0, tiled=True)
    cot_full = lax.all_gather(cot_rows, "tensor", axis=0, tiled=True)

    gate_in = dot_wide(normed, w_gate)
    side_out = dot_wide(normed, w_side)
    pre = jnp.concatenate([dot_wide(normed, w_mix), side_out[:, :bc_size]], axis=1).astype(low)
    raw_dt = side_out[:, bc_size : bc_size + PAD] + local_bias
    step_dt = jax.nn.softplus(raw_dt)
    rate = -jnp.exp(local_log) * (jnp.arange(PAD) < heads_here)
    log_decay = step_dt * rate

    tail_start = token_count - width_back
    own_tail = jnp.concatenate(
        [pre[tail_start:], segments[tail_start:, None].astype(low)], axis=1
    )
    tail = from_behind(own_tail, "dp", 1)
    tail_vals, tail_ids = tail[:, :-1], tail[:, -1].astype(jnp.int32)
    seg_ext = jnp.concatenate([tail_ids, segments])
    pos_ext = (
        data_index * token_count
        - width_back
        + jnp.arange(token_count + width_back, dtype=jnp.int32)
    )
    sequences = data_count * token_count // LENGTH + 1
    key_ext = seg_ext * sequences + pos_ext // LENGTH
    key = key_ext[width_back:]
    before = key_ext[width_back - 1 : width_back].reshape(1, 1)
    validity = jnp.stack(
        [key_ext[k : k + token_count] == key for k in range(width_back + 1)], axis=1
    ).astype(jnp.float32)
    pre_ext = jnp.concatenate([tail_vals, pre], axis=0).astype(jnp.float32)
    activ = conv_apply(pre_ext, conv_weight, conv_bias, validity).astype(low)
    inner_x = activ[:, :inner_here]
    state_b = activ[:, inner_here : inner_here + state_size]
    state_c = activ[:, inner_here + state_size :]
    scan_args = (
        step_dt, step_dt.T, log_decay, log_decay.T, key[:, None], key[None, :], before,
    )
    local_y, local_end, inflow = scan_forward(
        inner_x, state_b, state_c, *scan_args, heads=heads_here
    )

    group = max(1, LENGTH // token_count)
    if data_count % group:
        group = data_count
    mine = data_index % group

    device_decay = jnp.repeat(inflow[-1].reshape(heads_here, head_size)[:, :1], state_size, axis=1)
    sent = jnp.concatenate([local_end.astype(low), pad_to(device_decay, 16, 0).astype(low)])
    arrived = spread(sent, "dp", group, 1)
    decays = jnp.repeat(
        arrived[:, inner_here : inner_here + heads_here].astype(jnp.float32), head_size, axis=1
    )
    entry_state = chain(arrived[:, :inner_here], decays, mine, False)
    x_wide = inner_x.astype(jnp.float32)
    mixed = (
        local_y + dot_wide(state_c, entry_state.T.astype(low)) * inflow + skip_wide * x_wide
    )
    sigm = jax.nn.sigmoid(gate_in)
    gate_act = gate_in * sigm
    gated = mixed * gate_act
    d_normed_out = dot_wide(cot_full, w_out)
    scaled = local_gate_gain * d_normed_out
    sums = jnp.stack([jnp.sum(gated * gated, axis=1), jnp.sum(scaled * gated, axis=1)])
    sums = lax.psum(sums, "tensor") / inner_total
    rstd_gate = lax.rsqrt(sums[0] + EPSILON)[:, None]
    gate_dots = sums[1][:, None]
    gated_normed = gated * rstd_gate
    normed_out = (gated_normed * local_gate_gain).astype(low)
    d_gated = rstd_gate * scaled - gated * rstd_gate**3 * gate_dots
    d_mixed = d_gated * gate_act
    d_gate_in = (d_gated * mixed * sigm * (1.0 + gate_in * (1.0 - sigm))).astype(low)
    branch = dot_wide(normed_out, w_out.T).astype(low)
    g_out = dot_wide(cot_full.T, normed_out).astype(low)
    state_cot = dot_wide((d_mixed * inflow).T.astype(low), state_c).astype(low)
    branch, g_out, state_cot = lax.optimization_barrier((branch, g_out, state_cot))
    branch = lax.psum_scatter(branch, "tensor", scatter_dimension=0, tiled=True)
    result = block_input + branch.astype(jnp.float32)
    g_out = lax.psum_scatter(g_out, "dp", scatter_dimension=0, tiled=True)
    cots = spread(state_cot, "dp", group, 2)
    leave_cot = chain(cots, decays, mine, True)
    g_gate_local = jnp.sum(d_normed_out * gated_normed, axis=0)
    g_skip_wide = jnp.sum(d_mixed * x_wide, axis=0)
    g_skip_local = jnp.sum(g_skip_wide.reshape(heads_here, head_size), axis=1)
    g_gate_in = dot_wide(normed.T, d_gate_in).astype(low)
    leave_cot, g_gate_in = lax.optimization_barrier((leave_cot, g_gate_in))
    g_gate_in = lax.psum_scatter(g_gate_in, "dp", scatter_dimension=0, tiled=True)

    d_x, d_b, d_c, dcum, colt, const, sx = scan_backward(
        inner_x, state_b, state_c, d_mixed, *scan_args, skip_wide, entry_state, leave_cot,
        heads=heads_here,
    )
    d_bc = lax.psum(jnp.concatenate([d_b, d_c], axis=1).astype(low), "tensor")
    d_step, d_log = step_gradients(dcum, colt, const, sx, log_decay, rate)
    ext_x, ext_bc = pre_ext[:, :inner_here], pre_ext[:, inner_here:]

    def conv_part(values, kernel, offsets):
        return conv_apply(values, kernel, offsets, validity)

    def shifted_back(ext, cols, d_out, axis_name):
        _, back = jax.vjp(conv_part, ext, conv_weight[:, cols], conv_bias[cols])
        d_ext, d_kernel, d_offsets = back(d_out)
        from_next = from_behind(d_ext[:width_back], axis_name, -1)
        own = d_ext[width_back:]
        own = jnp.concatenate([own[:tail_start], own[tail_start:] + from_next], axis=0)
        return own.astype(low), d_kernel, d_offsets

    d_mix, g_cxw_local, g_cxb_local = shifted_back(ext_x, slice(0, inner_here), d_x, "dp")
    d_pre_bc, g_cbw_local, g_cbb_local = shifted_back(
        ext_bc, slice(inner_here, None), d_bc.astype(jnp.float32), "dp"
    )
    d_raw = d_step * jax.nn.sigmoid(raw_dt)
    g_dt_bias_local = jnp.sum(d_raw, axis=0)
    d_raw_b = d_raw.astype(low)
    d_side = jnp.concatenate([d_pre_bc, d_raw_b], axis=1)
    partial_rows = (
        dot_wide(d_gate_in, w_gate.T)
        + dot_wide(d_mix, w_mix.T)
        + dot_wide(d_raw_b, w_side[:, bc_size : bc_size + PAD].T)
    )
    own_bc = lax.dynamic_slice_in_dim(d_pre_bc, tensor_index * row_count, row_count, 0)
    d_normed_rows = lax.psum_scatter(
        partial_rows.astype(low), "tensor", scatter_dimension=0, tiled=True
    ).astype(jnp.float32) + dot_wide(own_bc, w_side[:, :bc_size].T)
    g_in = dot_wide(normed.T, jnp.concatenate([d_mix, d_side], axis=1)).astype(low)
    g_in = pad_to(g_in, -(-g_in.shape[1] // 128) * 128, 1)
    g_in = lax.psum_scatter(g_in, "dp", scatter_dimension=0, tiled=True).astype(jnp.float32)
    grad_zx = jnp.stack([g_gate_in.astype(jnp.float32), g_in[:, :inner_here]])
    side_end = inner_here + bc_size
    grad_bc = g_in[:, inner_here:side_end]
    grad_dt = g_in[:, side_end : side_end + heads_here]
    grad_out = g_out.astype(jnp.float32).T
    scaled_in = norm_gain * d_normed_rows
    g_norm_local = jnp.sum(d_normed_rows * block_input * rstd, axis=0)
    grad_input = (
        cotangent
        + rstd * scaled_in
        - block_input * rstd**3 * jnp.mean(scaled_in * block_input, axis=-1, keepdims=True)
    )
    pieces = (
        g_cxw_local,
        g_cxb_local,
        g_gate_local,
        g_dt_bias_local[:heads_here],
        d_log[:heads_here],
        g_skip_local,
        g_norm_local,
        g_cbw_local,
        g_cbb_local,
    )
    flat = jnp.concatenate([piece.reshape(-1) for piece in pieces])
    flat = pad_to(flat, -(-flat.shape[0] // 1024) * 1024, 0).reshape(-1, 128)
    flat = jnp.sum(spread(flat, "dp", data_count, 3), axis=0)
    flat = spread(flat, "tensor", tensor_count, 4).reshape(tensor_count, -1)
    small, at = [], 0
    for piece in pieces:
        small.append(flat[:, at : at + piece.size].reshape((tensor_count,) + piece.shape))
        at += piece.size
    grad_cxw = jnp.moveaxis(small[0], 0, 1).reshape(-1, inner_total)
    grad_cxb, grad_gate, grad_dtb, grad_log, grad_skip = [
        part.reshape(-1) for part in small[1:6]
    ]
    grad_norm = jnp.sum(small[6], axis=0)
    grad_cbw, grad_cbb = small[7][0], small[8][0]
    return (
        result,
        grad_input,
        grad_norm,
        grad_zx,
        grad_bc,
        grad_dt,
        grad_cxw,
        grad_cxb,
        grad_cbw,
        grad_cbb,
        grad_dtb,
        grad_log,
        grad_skip,
        grad_gate,
        grad_out,
    )


def solution(mesh):
    in_specs = (
        P(("dp", "tensor"), None),
        P(),
        P(None, "dp", "tensor"),
        P("dp", None),
        P("dp", "tensor"),
        P(),
        P(),
        P(),
        P(),
        P(),
        P(),
        P(),
        P(),
        P("tensor", "dp"),
        P("dp"),
        P(("dp", "tensor"), None),
    )
    out_specs = (
        P(("dp", "tensor"), None),
        P(("dp", "tensor"), None),
        P(),
        P(None, "dp", "tensor"),
        P("dp", None),
        P("dp", "tensor"),
        P(),
        P(),
        P(),
        P(),
        P(),
        P(),
        P(),
        P(),
        P("tensor", "dp"),
    )

    return jax.shard_map(
        per_device, mesh=mesh, in_specs=in_specs, out_specs=out_specs, check_vma=False
    )
```
